32 devices in a mesh: dom: 8 (over z, core), group: 4 (over y, x).
Axes of the slice: x: 2, y: 2, z: 4, core: 2. Of those that a mesh axis runs over, the one named last changes fastest.
Arguments:
- start: bfloat16 [64, 32768], P(None, ('dom', 'group')), may hold values from -8.1 to 8.1
- tiles: int32 [32, 32, 128, 128], P(('dom', 'group')), may hold values from 0 to 15
- row_ptr: int32 [32, 9], P(('dom', 'group')), may hold values from 0 to 32, as said below
- col_part: int32 [32, 32], P(('dom', 'group')), may hold values from 0 to 7
- col_local: int32 [32, 32], P(('dom', 'group')), may hold values from 0 to 31, as said below
- halo_list: int32 [8, 8, 4], P('dom'), may hold values from 0 to 31
Outputs:
- vectors: bfloat16 [64, 32768], P(None, ('dom', 'group'))
- ritz: float32 [64, 64], replicated
The draws below stay inside these ranges and needn't reach their ends.
Inputs may be any that keep to these rules, and one draw needn't show every extreme that they name: `row_ptr`: each row is strictly increasing from 0, so every block row has one or more slots; its last entry is at most 32 and equals 32 on some device row. `col_local`: below 32 where col_part names the row's own partition, below 4 otherwise.
All inputs are finite; a program needn't handle non-finite values.
Results may differ from the reference program's by a relative error of at most 0.012.
Values may be sent and summed in bfloat16 or wider, within the bound.
A program may use at most 64 MiB of HBM per device.

```python
import math
import jax
import jax.numpy as jnp
from jax import lax

BLOCK = 128
K = 64
BR_DEV = 8
ITERS = 2
HALO = 4
SLOTS = 32
PARTITIONS = 8
SUBSHARDS = 4
NBP = 32
NB = 256
ROWS = 32768
N_DOM = 8
N_GROUP = 4


def draw_start(key, part):
    first, second, third, fourth = jax.random.split(jax.random.fold_in(key, 37), 4)
    shared = jnp.clip(jax.random.normal(first, (1, ROWS), jnp.float32), -3.0, 3.0)
    noise = jnp.clip(jax.random.normal(second, (K, ROWS), jnp.float32), -3.0, 3.0)
    scale = jnp.exp(jax.random.uniform(third, (K, 1), jnp.float32, math.log(0.5), math.log(2.0)))
    spread = 0.6
    sign = jnp.where(jax.random.randint(fourth, (K, 1), 0, 2) == 0, -1.0, 1.0).astype(jnp.float32)
    return (sign * scale * shared + spread * noise).astype(jnp.bfloat16)


def draw_row_ptr(key, part):
    first, second, third = jax.random.split(jax.random.fold_in(key, 11), 3)
    count = PARTITIONS * SUBSHARDS
    used = jax.random.randint(first, (count,), SLOTS // 4, SLOTS + 1)
    fullest = jax.random.randint(second, (), 0, count)
    used = jnp.where(jnp.arange(count) == fullest, SLOTS, used)
    spread = used // (8 * BR_DEV)
    noise = jax.random.randint(third, (count, BR_DEV - 1), 0, 1 << 20)
    jitter = noise % (2 * spread[:, None] + 1) - spread[:, None]
    inner = jnp.arange(1, BR_DEV)[None, :] * used[:, None] // BR_DEV + jitter
    zeros = jnp.zeros((count, 1), jnp.int32)
    return jnp.concatenate([zeros, inner.astype(jnp.int32), used[:, None].astype(jnp.int32)], axis=1).astype(jnp.int32)


def link_draw(key):
    first, second, third, fourth = jax.random.split(jax.random.fold_in(key, 23), 4)
    count = PARTITIONS * SUBSHARDS
    own = (jnp.arange(count, dtype=jnp.int32) // SUBSHARDS)[:, None]
    remote = jax.random.randint(first, (count, SLOTS), 0, 4) == 0
    other = (own + jax.random.randint(second, (count, SLOTS), 1, PARTITIONS)) % PARTITIONS
    parts = jnp.where(remote, other, own).astype(jnp.int32)
    places = jnp.where(remote, jax.random.randint(third, (count, SLOTS), 0, HALO), jax.random.randint(fourth, (count, SLOTS), 0, NBP))
    return (parts, places.astype(jnp.int32))


def draw_col_part(key, part):
    return link_draw(key)[0]


def draw_col_local(key, part):
    return link_draw(key)[1]


def plant(values, stream_key, low, top_value):
    longest = values.shape.index(max(values.shape))
    spots = []
    for shift in (0, 1):
        where = [jax.random.randint(jax.random.fold_in(stream_key, axis), (), 0, length) for axis, length in enumerate(values.shape)]
        where[longest] = (where[longest] + shift) % values.shape[longest]
        spots.append(tuple(where))
    return values.at[spots[0]].set(low).at[spots[1]].set(top_value)


def setup_inputs(seed: int = 0) -> dict:
    splits = jax.random.split(jax.random.key(seed), 7)
    return {
        "start": draw_start(jax.random.fold_in(splits[6], 71), 0),
        "tiles": plant(jax.random.randint(splits[1], (N_DOM * N_GROUP, SLOTS, BLOCK, BLOCK), 0, 16), jax.random.fold_in(splits[1], 1), 0, 15).astype(jnp.int32),
        "row_ptr": draw_row_ptr(jax.random.fold_in(splits[6], 71), 0),
        "col_part": draw_col_part(jax.random.fold_in(splits[6], 71), 0),
        "col_local": draw_col_local(jax.random.fold_in(splits[6], 71), 0),
        "halo_list": plant(jax.random.randint(splits[5], (N_DOM, N_DOM, HALO), 0, NBP), jax.random.fold_in(splits[5], 1), 0, NBP - 1).astype(jnp.int32),
    }


def apply_graph(vectors, tiles, row_ptr, col_part, col_local, halo_list):
    blocked = vectors.astype(jnp.float32).reshape(K, NB, BLOCK)

    def one_row(entry):
        own = entry // SUBSHARDS
        pointers = row_ptr[entry]
        parts = col_part[entry]
        places = col_local[entry]
        remote = halo_list[parts, own, jnp.clip(places, 0, HALO - 1)]
        column = jnp.where(parts == own, own * NBP + places, parts * NBP + remote).astype(jnp.int32)
        picked = jnp.take(blocked, column, axis=1)
        centred = tiles[entry].astype(jnp.float32) - 7.5
        products = jnp.einsum('ksj,sij->ksi', picked, centred, precision=lax.Precision.HIGHEST)
        slot_ids = jnp.arange(SLOTS, dtype=jnp.int32)
        member = ((slot_ids[None, :] >= pointers[:-1, None]) & (slot_ids[None, :] < pointers[1:, None])).astype(jnp.float32)
        summed = jnp.einsum('rs,ksi->kri', member, products, precision=lax.Precision.HIGHEST)
        counts = (pointers[1:] - pointers[:-1]).astype(jnp.float32)
        return summed * (1.0 / (4.0 * jnp.sqrt(BLOCK * counts)))[None, :, None]
    result = lax.map(one_row, jnp.arange(PARTITIONS * SUBSHARDS, dtype=jnp.int32))
    return jnp.transpose(result, (1, 0, 2, 3)).reshape(K, ROWS)

def reference(start, tiles, row_ptr, col_part, col_local, halo_list):
    vectors = start
    for step in range(ITERS):
        image = apply_graph(vectors, tiles, row_ptr, col_part, col_local, halo_list)
        rounded = image.astype(jnp.bfloat16)
        gram = jnp.dot(rounded.astype(jnp.float32), rounded.T.astype(jnp.float32), preferred_element_type=jnp.float32) / ROWS
        lower = jnp.linalg.cholesky(gram)
        vectors = lax.linalg.triangular_solve(lower, rounded.astype(jnp.float32), left_side=True, lower=True).astype(jnp.bfloat16)
    final = apply_graph(vectors, tiles, row_ptr, col_part, col_local, halo_list)
    ritz = jnp.dot(vectors.astype(jnp.float32), final.T, precision=lax.Precision.HIGHEST) / ROWS
    return (vectors, ritz)
```

```python
import functools

import jax
import jax.numpy as jnp
from jax import lax
from jax.experimental import pallas as pl
from jax.experimental.pallas import tpu as pltpu
from jax.sharding import PartitionSpec as P

ITERS = 2
MESH = pl.DeviceIdType.MESH
HIGH = lax.Precision.HIGHEST
CHUNK = 8


def dot(a, b, dims=((1,), (0,)), precision=None):
    return lax.dot_general(a, b, (dims, ((), ())), precision=precision, preferred_element_type=jnp.float32)


def inverse_factor(gram):
    k = gram.shape[0]
    rows = lax.broadcasted_iota(jnp.int32, (k, k), 0)
    cols = lax.broadcasted_iota(jnp.int32, (k, k), 1)
    work = jnp.concatenate([gram, jnp.where(rows == cols, 1.0, 0.0).astype(jnp.float32)], axis=1)
    row_ids = lax.broadcasted_iota(jnp.int32, (k, 1), 0)
    pivots = jnp.zeros((k, 1), jnp.float32)
    for i in range(k):
        column = work[:, i : i + 1]
        pivot = work[i : i + 1, i : i + 1]
        pivots = jnp.where(row_ids == i, pivot, pivots)
        factor = jnp.where(row_ids > i, column / pivot, 0.0)
        work = work - factor * work[i : i + 1, :]
    return work[:, k:] * (1.0 / jnp.sqrt(pivots))


def kernel(n_dom, n_group, halo, total_rows, *refs):
    start_ref, tiles_ref, ptr_ref, cpart_ref, cloc_ref, halo_ref, vec_ref, ritz_ref = refs[:8]
    refs = refs[8:]
    n_apply = ITERS + 1
    parts, refs = refs[:n_apply], refs[n_apply:]
    halos, refs = refs[:n_apply], refs[n_apply:]
    stages, refs = refs[:n_apply], refs[n_apply:]
    raw, tb, prod, rounded_ref = refs[:4]
    refs = refs[4:]
    g_src, refs = refs[:n_apply], refs[n_apply:]
    g_one, refs = refs[:n_apply], refs[n_apply:]
    g_two, refs = refs[:n_apply], refs[n_apply:]
    g_all, refs = refs[:n_apply], refs[n_apply:]
    tile_sem, s1, r1, s2, r2, s3, r3, sa, ra, sb, rb, sc, rc = refs

    own = lax.axis_index("dom")
    me = lax.axis_index("group")
    slots, block = tb.shape[0], tb.shape[1]
    width = start_ref.shape[0]
    block_rows = start_ref.shape[1] // block
    per = max(1, halo // n_group)
    senders = halo // per
    gram_rows = width // n_group
    doms = []
    for step in range(1, n_dom // 2 + 1):
        doms.append(step)
        if n_dom - step != step:
            doms.append(n_dom - step)

    def up(offset):
        return lax.rem(own + offset, n_dom)

    def beside(offset):
        return lax.rem(me + offset, n_group)

    def as_sender(index, body):
        if senders == n_group:
            body()
        else:
            pl.when(index < senders)(body)

    def remote(src, dst, send_sem, recv_sem, device):
        return pltpu.make_async_remote_copy(
            src_ref=src, dst_ref=dst, send_sem=send_sem, recv_sem=recv_sem, device_id=device, device_id_type=MESH
        )

    barrier = pltpu.get_barrier_semaphore()
    for offset in range(1, n_group):
        pl.semaphore_signal(barrier, inc=1, device_id=(own, beside(offset)), device_id_type=MESH)
    for offset in range(1, n_dom):
        pl.semaphore_signal(barrier, inc=1, device_id=(up(offset), me), device_id_type=MESH)

    n_chunks = slots // CHUNK
    loads = [
        pltpu.make_async_copy(
            tiles_ref.at[0, pl.ds(c * CHUNK, CHUNK)], raw.at[pl.ds(c * CHUNK, CHUNK)], tile_sem.at[c]
        )
        for c in range(n_chunks)
    ]
    for load in loads:
        load.start()

    def put_own(a, values):
        for b in range(block_rows):
            parts[a][me * block_rows + b] = values[:, b * block : (b + 1) * block]

    def first_copies(a):
        mine = pl.ds(me * block_rows, block_rows)
        return [
            remote(parts[a].at[mine], parts[a].at[mine], s1.at[a, o], r1.at[a, o], (own, beside(o)))
            for o in range(1, n_group)
        ]

    def second_copies(a):
        place = pl.ds(own * halo + me * per, per)
        return [
            remote(stages[a].at[o], halos[a].at[place], s2.at[a, o], r2.at[a, o], (up(o), me)) for o in doms
        ]

    def third_copies(a, o):
        place = pl.ds(up(n_dom - o) * halo + me * per, per)
        return [
            remote(halos[a].at[place], halos[a].at[place], s3.at[a, o, j], r3.at[a, o, j], (own, beside(j)))
            for j in range(1, n_group)
        ]

    def exchange_second(a):
        for copy in first_copies(a):
            copy.wait_recv()

        def body():
            for o in doms:
                for h in range(per):
                    stages[a][o, h] = parts[a][halo_ref[0, up(o), me * per + h]]
            for copy in second_copies(a):
                copy.start()

        as_sender(me, body)

    def exchange_third(a):
        def body():
            for o, copy in zip(doms, second_copies(a)):
                copy.wait_recv()
                for spread in third_copies(a, o):
                    spread.start()

        as_sender(me, body)

    def exchange_end(a):
        for o in doms:
            for j, copy in zip(range(1, n_group), third_copies(a, o)):
                as_sender(beside(n_group - j), copy.wait_recv)

    def exchange_sends(a):
        for copy in first_copies(a):
            copy.wait_send()

        def body():
            for o, copy in zip(doms, second_copies(a)):
                copy.wait_send()
                for spread in third_copies(a, o):
                    spread.wait_send()

        as_sender(me, body)

    def apply_graph(a):
        prod[0] = jnp.zeros((width, block), jnp.float32)

        def body(c, total):
            for i in range(CHUNK):
                s = c * CHUNK + i
                here = cpart_ref[0, s] == own
                near = parts[a][jnp.where(here, cloc_ref[0, s], 0)]
                far = halos[a][jnp.where(here, 0, cpart_ref[0, s] * halo + cloc_ref[0, s])]
                picked = jnp.where(here, near, far)
                total = total + dot(picked, tb[s], ((1,), (1,)))
                prod[s + 1] = total
            return total

        lax.fori_loop(0, n_chunks, body, jnp.zeros((width, block), jnp.float32))
        out = []
        for r in range(block_rows):
            low, high = ptr_ref[0, r], ptr_ref[0, r + 1]
            count = jnp.full((1, block), high - low, jnp.int32).astype(jnp.float32)
            scale = 1.0 / (4.0 * jnp.sqrt(block * count))
            out.append((prod[high] - prod[low]) * scale)
        return jnp.concatenate(out, axis=1)

    def sum_one(t, value):
        padded = jnp.concatenate([value, jnp.zeros((width, block - width), jnp.float32)], axis=1)
        g_src[t][...] = padded.reshape(n_group, gram_rows, block)
        g_one[t][me] = g_src[t][me]
        copies = [
            remote(g_src[t].at[beside(o)], g_one[t].at[me], sa.at[t, o], ra.at[t, o], (own, beside(o)))
            for o in range(1, n_group)
        ]
        for copy in copies:
            copy.start()
        return copies

    def sum_two(t, copies):
        for copy in copies:
            copy.wait_recv()
        total = g_one[t][0]
        for j in range(1, n_group):
            total = total + g_one[t][j]
        g_two[t][own] = total
        more = [
            remote(g_two[t].at[own], g_two[t].at[own], sb.at[t, o], rb.at[t, o], (up(o), me)) for o in doms
        ]
        for copy in more:
            copy.start()
        return more

    def sum_three(t, copies):
        for copy in copies:
            copy.wait_recv()
        total = g_two[t][0]
        for j in range(1, n_dom):
            total = total + g_two[t][j]
        g_all[t][me] = total * (1.0 / total_rows)
        more = [
            remote(g_all[t].at[me], g_all[t].at[me], sc.at[t, o], rc.at[t, o], (own, beside(o)))
            for o in range(1, n_group)
        ]
        for copy in more:
            copy.start()
        return more

    def sum_end(t, copies):
        for copy in copies:
            copy.wait_recv()
        return g_all[t][...].reshape(width, block)[:, :width]

    put_own(0, start_ref[...])
    pl.semaphore_wait(barrier, n_group - 1 + n_dom - 1)
    for copy in first_copies(0):
        copy.start()

    for c, load in enumerate(loads):
        load.wait()

        def convert(i, carry):
            s = c * CHUNK + i
            tb[s] = (raw[s].astype(jnp.float32) - 7.5).astype(jnp.bfloat16)
            return carry

        lax.fori_loop(0, CHUNK, convert, 0)

    exchange_second(0)
    exchange_third(0)
    exchange_end(0)

    pending = []
    inverse = None
    for t in range(ITERS):
        image = apply_graph(t)
        if t > 0:
            image = dot(inverse, image, precision=HIGH)
        rounded = image.astype(jnp.bfloat16)
        put_own(t + 1, rounded)
        for copy in first_copies(t + 1):
            copy.start()
        rounded_ref[...] = rounded
        one = sum_one(t, dot(rounded, rounded, ((1,), (1,))))
        exchange_second(t + 1)
        two = sum_two(t, one)
        exchange_third(t + 1)
        three = sum_three(t, two)
        inverse = inverse_factor(sum_end(t, three))
        pending += one + two + three
        if t == ITERS - 1:
            vectors = dot(inverse, rounded_ref[...].astype(jnp.float32), precision=HIGH).astype(jnp.bfloat16)
            vec_ref[...] = vectors
        exchange_end(t + 1)

    final = dot(inverse, apply_graph(ITERS), precision=HIGH)
    local = dot(vec_ref[...].astype(jnp.float32), final, ((1,), (1,)), precision=HIGH)
    one = sum_one(ITERS, local)
    two = sum_two(ITERS, one)
    three = sum_three(ITERS, two)
    ritz_ref[...] = sum_end(ITERS, three)
    pending += one + two + three
    for copy in pending:
        copy.wait_send()
    for a in range(n_apply):
        exchange_sends(a)


def solution(mesh):
    n_dom, n_group = mesh.shape["dom"], mesh.shape["group"]
    n_apply = ITERS + 1

    def step(start, tiles, row_ptr, col_part, col_local, halo_list):
        width, rows_dev = start.shape
        slots, block = tiles.shape[1], tiles.shape[2]
        halo = halo_list.shape[2]
        in_part = rows_dev // block * n_group
        per = max(1, halo // n_group)
        gram_rows = width // n_group
        vmem = pl.BlockSpec(memory_space=pltpu.VMEM)
        smem = pl.BlockSpec(memory_space=pltpu.SMEM)
        dma = pltpu.SemaphoreType.DMA
        return pl.pallas_call(
            functools.partial(kernel, n_dom, n_group, halo, rows_dev * n_dom * n_group),
            out_shape=(
                jax.ShapeDtypeStruct((width, rows_dev), jnp.bfloat16),
                jax.ShapeDtypeStruct((width, width), jnp.float32),
            ),
            in_specs=[vmem, pl.BlockSpec(memory_space=pl.ANY), smem, smem, smem, smem],
            out_specs=(vmem, vmem),
            scratch_shapes=(
                [pltpu.VMEM((in_part, width, block), jnp.bfloat16)] * n_apply
                + [pltpu.VMEM((n_dom * halo, width, block), jnp.bfloat16)] * n_apply
                + [pltpu.VMEM((n_dom, per, width, block), jnp.bfloat16)] * n_apply
                + [
                    pltpu.VMEM((slots, block, block), jnp.int32),
                    pltpu.VMEM((slots, block, block), jnp.bfloat16),
                    pltpu.VMEM((slots + 1, width, block), jnp.float32),
                    pltpu.VMEM((width, rows_dev), jnp.bfloat16),
                ]
                + [pltpu.VMEM((n_group, gram_rows, block), jnp.float32)] * n_apply
                + [pltpu.VMEM((n_group, gram_rows, block), jnp.float32)] * n_apply
                + [pltpu.VMEM((n_dom, gram_rows, block), jnp.float32)] * n_apply
                + [pltpu.VMEM((n_group, gram_rows, block), jnp.float32)] * n_apply
                + [dma((slots // CHUNK,))]
                + [dma((n_apply, n_group))] * 2
                + [dma((n_apply, n_dom))] * 2
                + [dma((n_apply, n_dom, n_group))] * 2
                + [dma((n_apply, n_group))] * 2
                + [dma((n_apply, n_dom))] * 2
                + [dma((n_apply, n_group))] * 2
            ),
            compiler_params=pltpu.CompilerParams(
                collective_id=0, has_side_effects=True, vmem_limit_bytes=48 * 1024 * 1024
            ),
        )(start, tiles, row_ptr, col_part, col_local, halo_list)

    return jax.shard_map(
        step,
        mesh=mesh,
        in_specs=(
            P(None, ("dom", "group")),
            P(("dom", "group"), None, None, None),
            P(("dom", "group"), None),
            P(("dom", "group"), None),
            P(("dom", "group"), None),
            P("dom", None, None),
        ),
        out_specs=(P(None, ("dom", "group")), P()),
        check_vma=False,
    )
```

```python
import functools

import jax
import jax.numpy as jnp
from jax import lax
from jax.experimental import pallas as pl
from jax.experimental.pallas import tpu as pltpu
from jax.sharding import PartitionSpec as P

ITERS = 2
MESH = pl.DeviceIdType.MESH
HIGH = lax.Precision.HIGHEST
CHUNK = 8
PANEL = 4


def dot(a, b, dims=((1,), (0,)), precision=None):
    return lax.dot_general(a, b, (dims, ((), ())), precision=precision, preferred_element_type=jnp.float32)


def factor_start(gram):
    k = gram.shape[0]
    rows = lax.broadcasted_iota(jnp.int32, (k, k), 0)
    cols = lax.broadcasted_iota(jnp.int32, (k, k), 1)
    work = jnp.concatenate([gram, jnp.where(rows == cols, 1.0, 0.0).astype(jnp.float32)], axis=1)
    return work, jnp.ones(work.shape, jnp.float32)


def factor_steps(state, first, last):
    work, pivots = state
    row_ids = lax.broadcasted_iota(jnp.int32, work.shape, 0)
    for i in range(first, last, PANEL):
        cols = [jnp.broadcast_to(work[:, i + b : i + b + 1], work.shape) for b in range(PANEL)]
        rows = [work[i + b : i + b + 1, :] for b in range(PANEL)]
        for b in range(PANEL):
            pivot = cols[b][i + b : i + b + 1, :]
            inv = 1.0 / pivot
            pivots = jnp.where(row_ids == i + b, pivot, pivots)
            for c in range(b + 1, PANEL):
                ratio = cols[c][i + b : i + b + 1, :] * inv
                rows[c] = rows[c] - (cols[b][i + c : i + c + 1, :] * inv) * rows[b]
                cols[c] = cols[c] - cols[b] * ratio
            work = work - jnp.where(row_ids > i + b, cols[b], 0.0) * (rows[b] * inv)
    return work, pivots


def factor_end(state):
    work, pivots = state
    k = work.shape[0]
    return work[:, k:] * (1.0 / jnp.sqrt(pivots[:, k:]))


def kernel(n_dom, n_group, halo, total_rows, *refs):
    start_hbm, tiles_ref, ptr_hbm, cpart_hbm, cloc_hbm, halo_hbm, vec_ref, ritz_ref = refs[:8]
    start_ref, ptr_ref, cpart_ref, cloc_ref, halo_ref, in_sem = refs[8:14]
    refs = refs[14:]
    n_apply = ITERS + 1
    parts, refs = refs[:n_apply], refs[n_apply:]
    halos, refs = refs[:n_apply], refs[n_apply:]
    stages, refs = refs[:n_apply], refs[n_apply:]
    raw, tb, prod, rounded_ref = refs[:4]
    refs = refs[4:]
    g_src, refs = refs[:n_apply], refs[n_apply:]
    g_one, refs = refs[:n_apply], refs[n_apply:]
    g_two, refs = refs[:n_apply], refs[n_apply:]
    g_all, refs = refs[:n_apply], refs[n_apply:]
    tile_sem, s1, r1, s2, r2, s3, r3, sa, ra, sb, rb, sc, rc = refs

    own = lax.axis_index("dom")
    me = lax.axis_index("group")
    slots, block = tb.shape[0], tb.shape[1]
    width = start_ref.shape[0]
    block_rows = start_ref.shape[1] // block
    per = max(1, halo // n_group)
    senders = halo // per
    gram_rows = width // n_group
    doms = []
    for step in range(1, n_dom // 2 + 1):
        doms.append(step)
        if n_dom - step != step:
            doms.append(n_dom - step)

    def up(offset):
        return lax.rem(own + offset, n_dom)

    def beside(offset):
        return lax.rem(me + offset, n_group)

    def as_sender(index, body):
        if senders == n_group:
            body()
        else:
            pl.when(index < senders)(body)

    def remote(src, dst, send_sem, recv_sem, device):
        return pltpu.make_async_remote_copy(
            src_ref=src, dst_ref=dst, send_sem=send_sem, recv_sem=recv_sem, device_id=device, device_id_type=MESH
        )

    smalls = [
        pltpu.make_async_copy(src, dst, in_sem.at[i])
        for i, (src, dst) in enumerate(
            [
                (start_hbm, start_ref),
                (ptr_hbm, ptr_ref),
                (cpart_hbm, cpart_ref),
                (cloc_hbm, cloc_ref),
                (halo_hbm, halo_ref),
            ]
        )
    ]
    for load in smalls:
        load.start()

    barrier = pltpu.get_barrier_semaphore()
    for offset in range(1, n_group):
        pl.semaphore_signal(barrier, inc=1, device_id=(own, beside(offset)), device_id_type=MESH)
    for offset in range(1, n_dom):
        pl.semaphore_signal(barrier, inc=1, device_id=(up(offset), me), device_id_type=MESH)

    n_chunks = slots // CHUNK
    loads = [
        pltpu.make_async_copy(
            tiles_ref.at[0, pl.ds(c * CHUNK, CHUNK)], raw.at[pl.ds(c * CHUNK, CHUNK)], tile_sem.at[c]
        )
        for c in range(n_chunks)
    ]
    for load in loads:
        load.start()

    def put_own(a, values):
        for b in range(block_rows):
            parts[a][me * block_rows + b] = values[:, b * block : (b + 1) * block]

    relayed = n_group == 4
    half = block_rows // 2
    across = me + 1 - 2 * lax.rem(me, 2)
    along = beside(n_group // 2)

    def half_copy(a, who, part, index, to):
        place = pl.ds(who * block_rows + part * half, half)
        return remote(parts[a].at[place], parts[a].at[place], s1.at[a, index], r1.at[a, index], (own, to))

    def first_copies(a):
        if relayed:
            return [
                half_copy(a, me, 0, 0, across),
                half_copy(a, me, 1, 1, along),
                half_copy(a, me, 1, 2, across),
                half_copy(a, me, 0, 3, along),
            ]
        mine = pl.ds(me * block_rows, block_rows)
        return [
            remote(parts[a].at[mine], parts[a].at[mine], s1.at[a, o], r1.at[a, o], (own, beside(o)))
            for o in range(1, n_group)
        ]

    def relay_copies(a):
        return [half_copy(a, across, 0, 4, along), half_copy(a, along, 1, 5, across)]

    def exchange_relay(a):
        if relayed:
            for copy, relay in zip(first_copies(a)[:2], relay_copies(a)):
                copy.wait_recv()
                relay.start()

    def second_copies(a):
        place = pl.ds(own * halo + me * per, per)
        return [
            remote(stages[a].at[o], halos[a].at[place], s2.at[a, o], r2.at[a, o], (up(o), me)) for o in doms
        ]

    def third_copy(a, o, who, index, to):
        place = pl.ds(up(n_dom - o) * halo + who * per, per)
        return remote(halos[a].at[place], halos[a].at[place], s3.at[a, o, index], r3.at[a, o, index], (own, to))

    def third_copies(a, o):
        if relayed:
            return [third_copy(a, o, me, 0, across), third_copy(a, o, me, 1, along)]
        return [third_copy(a, o, me, j, beside(j)) for j in range(1, n_group)]

    def third_relay(a, o):
        if doms.index(o) % 2:
            return third_copy(a, o, along, 2, across)
        return third_copy(a, o, across, 2, along)

    def exchange_second(a):
        rest = first_copies(a)[2:] + relay_copies(a) if relayed else first_copies(a)
        for copy in rest:
            copy.wait_recv()

        def body():
            for o in doms:
                for h in range(per):
                    stages[a][o, h] = parts[a][halo_ref[0, up(o), me * per + h]]
            for copy in second_copies(a):
                copy.start()

        as_sender(me, body)

    def exchange_third(a):
        def body():
            for o, copy in zip(doms, second_copies(a)):
                copy.wait_recv()
                for spread in third_copies(a, o):
                    spread.start()

        as_sender(me, body)

    def exchange_end(a):
        if relayed:
            for o in doms:
                for copy in third_copies(a, o):
                    copy.wait_recv()
                third_relay(a, o).start()
            for o in doms:
                third_relay(a, o).wait_recv()
            return
        for o in doms:
            for j, copy in zip(range(1, n_group), third_copies(a, o)):
                as_sender(beside(n_group - j), copy.wait_recv)

    def exchange_sends(a):
        for copy in first_copies(a) + (relay_copies(a) if relayed else []):
            copy.wait_send()

        def body():
            for o, copy in zip(doms, second_copies(a)):
                copy.wait_send()
                for spread in third_copies(a, o):
                    spread.wait_send()
                if relayed:
                    third_relay(a, o).wait_send()

        as_sender(me, body)

    def apply_graph(a):
        prod[0] = jnp.zeros((width, block), jnp.float32)

        def body(c, total):
            for i in range(CHUNK):
                s = c * CHUNK + i
                here = cpart_ref[0, s] == own
                near = parts[a][jnp.where(here, cloc_ref[0, s], 0)]
                far = halos[a][jnp.where(here, 0, cpart_ref[0, s] * halo + cloc_ref[0, s])]
                picked = jnp.where(here, near, far)
                total = total + dot(picked, tb[s], ((1,), (1,)))
                prod[s + 1] = total
            return total

        lax.fori_loop(0, n_chunks, body, jnp.zeros((width, block), jnp.float32))
        out = []
        for r in range(block_rows):
            low, high = ptr_ref[0, r], ptr_ref[0, r + 1]
            count = jnp.full((1, block), high - low, jnp.int32).astype(jnp.float32)
            scale = 1.0 / (4.0 * jnp.sqrt(block * count))
            out.append((prod[high] - prod[low]) * scale)
        return jnp.concatenate(out, axis=1)

    def sum_one(t, value):
        padded = jnp.concatenate([value, jnp.zeros((width, block - width), jnp.float32)], axis=1)
        g_src[t][...] = padded.reshape(n_group, gram_rows, block)
        g_one[t][me] = g_src[t][me]
        copies = [
            remote(g_src[t].at[beside(o)], g_one[t].at[me], sa.at[t, o], ra.at[t, o], (own, beside(o)))
            for o in range(1, n_group)
        ]
        for copy in copies:
            copy.start()
        return copies

    def sum_two(t, copies):
        for copy in copies:
            copy.wait_recv()
        total = g_one[t][0]
        for j in range(1, n_group):
            total = total + g_one[t][j]
        g_two[t][own] = total
        more = [
            remote(g_two[t].at[own], g_two[t].at[own], sb.at[t, o], rb.at[t, o], (up(o), me)) for o in doms
        ]
        for copy in more:
            copy.start()
        return more

    def sum_three(t, copies):
        for copy in copies:
            copy.wait_recv()
        total = g_two[t][0]
        for j in range(1, n_dom):
            total = total + g_two[t][j]
        g_all[t][me] = total * (1.0 / total_rows)
        more = [
            remote(g_all[t].at[me], g_all[t].at[me], sc.at[t, o], rc.at[t, o], (own, beside(o)))
            for o in range(1, n_group)
        ]
        for copy in more:
            copy.start()
        return more

    def sum_end(t, copies):
        for copy in copies:
            copy.wait_recv()
        return g_all[t][...].reshape(width, block)[:, :width]

    for load in smalls:
        load.wait()
    put_own(0, start_ref[...])
    pl.semaphore_wait(barrier, n_group - 1 + n_dom - 1)
    for copy in first_copies(0):
        copy.start()

    for c, load in enumerate(loads):
        load.wait()
        if c == n_chunks // 2:
            exchange_relay(0)

        def convert(i, carry):
            s = c * CHUNK + i
            tb[s] = (raw[s].astype(jnp.float32) - 7.5).astype(jnp.bfloat16)
            return carry

        lax.fori_loop(0, CHUNK, convert, 0)

    exchange_second(0)
    exchange_third(0)
    exchange_end(0)

    pending = []
    inverse = None
    for t in range(ITERS):
        image = apply_graph(t)
        if t > 0:
            image = dot(inverse, image, precision=HIGH)
        rounded = image.astype(jnp.bfloat16)
        put_own(t + 1, rounded)
        rounded_ref[...] = rounded
        one = sum_one(t, dot(rounded, rounded, ((1,), (1,))))
        for copy in first_copies(t + 1):
            copy.start()
        two = sum_two(t, one)
        exchange_relay(t + 1)
        three = sum_three(t, two)
        exchange_second(t + 1)
        state = factor_start(sum_end(t, three))
        state = factor_steps(state, 0, width // 2)
        exchange_third(t + 1)
        inverse = factor_end(factor_steps(state, width // 2, width))
        pending += one + two + three
        if t == ITERS - 1:
            vectors = dot(inverse, rounded_ref[...].astype(jnp.float32), precision=HIGH).astype(jnp.bfloat16)
            vec_ref[...] = vectors
        exchange_end(t + 1)

    final = dot(inverse, apply_graph(ITERS), precision=HIGH)
    local = dot(vec_ref[...].astype(jnp.float32), final, ((1,), (1,)), precision=HIGH)
    one = sum_one(ITERS, local)
    two = sum_two(ITERS, one)
    three = sum_three(ITERS, two)
    ritz_ref[...] = sum_end(ITERS, three)
    pending += one + two + three
    for copy in pending:
        copy.wait_send()
    for a in range(n_apply):
        exchange_sends(a)


def solution(mesh):
    n_dom, n_group = mesh.shape["dom"], mesh.shape["group"]
    n_apply = ITERS + 1

    def step(start, tiles, row_ptr, col_part, col_local, halo_list):
        width, rows_dev = start.shape
        slots, block = tiles.shape[1], tiles.shape[2]
        halo = halo_list.shape[2]
        in_part = rows_dev // block * n_group
        per = max(1, halo // n_group)
        gram_rows = width // n_group
        vmem = pl.BlockSpec(memory_space=pltpu.VMEM)
        dma = pltpu.SemaphoreType.DMA
        return pl.pallas_call(
            functools.partial(kernel, n_dom, n_group, halo, rows_dev * n_dom * n_group),
            out_shape=(
                jax.ShapeDtypeStruct((width, rows_dev), jnp.bfloat16),
                jax.ShapeDtypeStruct((width, width), jnp.float32),
            ),
            in_specs=[pl.BlockSpec(memory_space=pltpu.HBM)] * 6,
            out_specs=(vmem, vmem),
            scratch_shapes=(
                [
                    pltpu.VMEM(start.shape, start.dtype),
                    pltpu.SMEM(row_ptr.shape, jnp.int32),
                    pltpu.SMEM(col_part.shape, jnp.int32),
                    pltpu.SMEM(col_local.shape, jnp.int32),
                    pltpu.SMEM(halo_list.shape, jnp.int32),
                    dma((5,)),
                ]
                + [pltpu.VMEM((in_part, width, block), jnp.bfloat16)] * n_apply
                + [pltpu.VMEM((n_dom * halo, width, block), jnp.bfloat16)] * n_apply
                + [pltpu.VMEM((n_dom, per, width, block), jnp.bfloat16)] * n_apply
                + [
                    pltpu.VMEM((slots, block, block), jnp.int32),
                    pltpu.VMEM((slots, block, block), jnp.bfloat16),
                    pltpu.VMEM((slots + 1, width, block), jnp.float32),
                    pltpu.VMEM((width, rows_dev), jnp.bfloat16),
                ]
                + [pltpu.VMEM((n_group, gram_rows, block), jnp.float32)] * n_apply
                + [pltpu.VMEM((n_group, gram_rows, block), jnp.float32)] * n_apply
                + [pltpu.VMEM((n_dom, gram_rows, block), jnp.float32)] * n_apply
                + [pltpu.VMEM((n_group, gram_rows, block), jnp.float32)] * n_apply
                + [dma((slots // CHUNK,))]
                + [dma((n_apply, max(6, n_group)))] * 2
                + [dma((n_apply, n_dom))] * 2
                + [dma((n_apply, n_dom, n_group))] * 2
                + [dma((n_apply, n_group))] * 2
                + [dma((n_apply, n_dom))] * 2
                + [dma((n_apply, n_group))] * 2
            ),
            compiler_params=pltpu.CompilerParams(
                collective_id=0, has_side_effects=True, vmem_limit_bytes=48 * 1024 * 1024
            ),
        )(start, tiles, row_ptr, col_part, col_local, halo_list)

    return jax.shard_map(
        step,
        mesh=mesh,
        in_specs=(
            P(None, ("dom", "group")),
            P(("dom", "group"), None, None, None),
            P(("dom", "group"), None),
            P(("dom", "group"), None),
            P(("dom", "group"), None),
            P("dom", None, None),
        ),
        out_specs=(P(None, ("dom", "group")), P()),
        check_vma=False,
    )
```

```python
import functools

import jax
import jax.numpy as jnp
from jax import lax
from jax.experimental import pallas as pl
from jax.experimental.pallas import tpu as pltpu
from jax.sharding import PartitionSpec as P

ITERS = 2
MESH = pl.DeviceIdType.MESH
HIGH = lax.Precision.HIGHEST
CHUNK = 8
PANEL = 4


def dot(a, b, dims=((1,), (0,)), precision=None):
    return lax.dot_general(a, b, (dims, ((), ())), precision=precision, preferred_element_type=jnp.float32)


def factor_start(gram):
    k = gram.shape[0]
    rows = lax.broadcasted_iota(jnp.int32, (k, k), 0)
    cols = lax.broadcasted_iota(jnp.int32, (k, k), 1)
    work = jnp.concatenate([gram, jnp.where(rows == cols, 1.0, 0.0).astype(jnp.float32)], axis=1)
    return work, jnp.ones(work.shape, jnp.float32)


def factor_steps(state, first, last):
    work, pivots = state
    row_ids = lax.broadcasted_iota(jnp.int32, work.shape, 0)
    for i in range(first, last, PANEL):
        cols = [jnp.broadcast_to(work[:, i + b : i + b + 1], work.shape) for b in range(PANEL)]
        rows = [work[i + b : i + b + 1, :] for b in range(PANEL)]
        for b in range(PANEL):
            pivot = cols[b][i + b : i + b + 1, :]
            inv = 1.0 / pivot
            pivots = jnp.where(row_ids == i + b, pivot, pivots)
            for c in range(b + 1, PANEL):
                ratio = cols[c][i + b : i + b + 1, :] * inv
                rows[c] = rows[c] - (cols[b][i + c : i + c + 1, :] * inv) * rows[b]
                cols[c] = cols[c] - cols[b] * ratio
            work = work - jnp.where(row_ids > i + b, cols[b], 0.0) * (rows[b] * inv)
    return work, pivots


def factor_end(state):
    work, pivots = state
    k = work.shape[0]
    return work[:, k:] * (1.0 / jnp.sqrt(pivots[:, k:]))


def kernel(n_dom, n_group, halo, total_rows, *refs):
    start_hbm, tiles_ref, ptr_hbm, cpart_hbm, cloc_hbm, halo_hbm, vec_ref, ritz_ref = refs[:8]
    start_ref, ptr_ref, cpart_ref, cloc_ref, halo_ref, in_sem = refs[8:14]
    refs = refs[14:]
    n_apply = ITERS + 1
    parts, refs = refs[:n_apply], refs[n_apply:]
    halos, refs = refs[:n_apply], refs[n_apply:]
    stages, refs = refs[:n_apply], refs[n_apply:]
    raw, tb, prod, rounded_ref = refs[:4]
    refs = refs[4:]
    g_src, refs = refs[:n_apply], refs[n_apply:]
    g_one, refs = refs[:n_apply], refs[n_apply:]
    g_two, refs = refs[:n_apply], refs[n_apply:]
    g_all, refs = refs[:n_apply], refs[n_apply:]
    tile_sem, s1, r1, s2, r2, s3, r3, sa, ra, sb, rb, sc, rc = refs

    own = lax.axis_index("dom")
    me = lax.axis_index("group")
    slots, block = tb.shape[0], tb.shape[1]
    width = start_ref.shape[0]
    block_rows = start_ref.shape[1] // block
    per = max(1, halo // n_group)
    senders = halo // per
    gram_rows = width // n_group
    doms = []
    for step in range(1, n_dom // 2 + 1):
        doms.append(step)
        if n_dom - step != step:
            doms.append(n_dom - step)

    def up(offset):
        return lax.rem(own + offset, n_dom)

    def beside(offset):
        return lax.rem(me + offset, n_group)

    def as_sender(index, body):
        if senders == n_group:
            body()
        else:
            pl.when(index < senders)(body)

    def remote(src, dst, send_sem, recv_sem, device):
        return pltpu.make_async_remote_copy(
            src_ref=src, dst_ref=dst, send_sem=send_sem, recv_sem=recv_sem, device_id=device, device_id_type=MESH
        )

    smalls = [
        pltpu.make_async_copy(src, dst, in_sem.at[i])
        for i, (src, dst) in enumerate(
            [
                (start_hbm, start_ref),
                (ptr_hbm, ptr_ref),
                (cpart_hbm, cpart_ref),
                (cloc_hbm, cloc_ref),
                (halo_hbm, halo_ref),
            ]
        )
    ]
    for load in smalls:
        load.start()

    barrier = pltpu.get_barrier_semaphore()
    for offset in range(1, n_group):
        pl.semaphore_signal(barrier, inc=1, device_id=(own, beside(offset)), device_id_type=MESH)
    for offset in range(1, n_dom):
        pl.semaphore_signal(barrier, inc=1, device_id=(up(offset), me), device_id_type=MESH)

    n_chunks = slots // CHUNK
    loads = [
        pltpu.make_async_copy(
            tiles_ref.at[0, pl.ds(c * CHUNK, CHUNK)], raw.at[pl.ds(c * CHUNK, CHUNK)], tile_sem.at[c]
        )
        for c in range(n_chunks)
    ]
    for load in loads:
        load.start()

    def put_own(a, values):
        for b in range(block_rows):
            parts[a][me * block_rows + b] = values[:, b * block : (b + 1) * block]

    relayed = n_group == 4
    half = block_rows // 2
    across = me + 1 - 2 * lax.rem(me, 2)
    along = beside(n_group // 2)

    def half_copy(a, who, part, index, to):
        place = pl.ds(who * block_rows + part * half, half)
        return remote(parts[a].at[place], parts[a].at[place], s1.at[a, index], r1.at[a, index], (own, to))

    def first_copies(a):
        if relayed:
            return [
                half_copy(a, me, 0, 0, across),
                half_copy(a, me, 1, 1, along),
                half_copy(a, me, 1, 2, across),
                half_copy(a, me, 0, 3, along),
            ]
        mine = pl.ds(me * block_rows, block_rows)
        return [
            remote(parts[a].at[mine], parts[a].at[mine], s1.at[a, o], r1.at[a, o], (own, beside(o)))
            for o in range(1, n_group)
        ]

    def relay_copies(a):
        return [half_copy(a, across, 0, 4, along), half_copy(a, along, 1, 5, across)]

    def exchange_relay(a):
        if relayed:
            for copy, relay in zip(first_copies(a)[:2], relay_copies(a)):
                copy.wait_recv()
                relay.start()

    def second_copies(a):
        place = pl.ds(own * halo + me * per, per)
        return [
            remote(stages[a].at[o], halos[a].at[place], s2.at[a, o], r2.at[a, o], (up(o), me)) for o in doms
        ]

    def third_copy(a, o, who, index, to):
        place = pl.ds(up(n_dom - o) * halo + who * per, per)
        return remote(halos[a].at[place], halos[a].at[place], s3.at[a, o, index], r3.at[a, o, index], (own, to))

    def third_copies(a, o):
        return [third_copy(a, o, me, j, beside(j)) for j in range(1, n_group)]

    def exchange_second(a):
        rest = first_copies(a)[2:] + relay_copies(a) if relayed else first_copies(a)
        for copy in rest:
            copy.wait_recv()

        def body():
            for o in doms:
                for h in range(per):
                    stages[a][o, h] = parts[a][halo_ref[0, up(o), me * per + h]]
            for copy in second_copies(a):
                copy.start()

        as_sender(me, body)

    def exchange_third(a):
        def body():
            for o, copy in zip(doms, second_copies(a)):
                copy.wait_recv()
                for spread in third_copies(a, o):
                    spread.start()

        as_sender(me, body)

    def exchange_end(a):
        for o in doms:
            for j, copy in zip(range(1, n_group), third_copies(a, o)):
                as_sender(beside(n_group - j), copy.wait_recv)

    def exchange_sends(a):
        for copy in first_copies(a) + (relay_copies(a) if relayed else []):
            copy.wait_send()

        def body():
            for o, copy in zip(doms, second_copies(a)):
                copy.wait_send()
                for spread in third_copies(a, o):
                    spread.wait_send()

        as_sender(me, body)

    def apply_graph(a):
        prod[0] = jnp.zeros((width, block), jnp.float32)

        def body(c, total):
            for i in range(CHUNK):
                s = c * CHUNK + i
                here = cpart_ref[0, s] == own
                near = parts[a][jnp.where(here, cloc_ref[0, s], 0)]
                far = halos[a][jnp.where(here, 0, cpart_ref[0, s] * halo + cloc_ref[0, s])]
                picked = jnp.where(here, near, far)
                total = total + dot(picked, tb[s], ((1,), (1,)))
                prod[s + 1] = total
            return total

        lax.fori_loop(0, n_chunks, body, jnp.zeros((width, block), jnp.float32))
        out = []
        for r in range(block_rows):
            low, high = ptr_ref[0, r], ptr_ref[0, r + 1]
            count = jnp.full((1, block), high - low, jnp.int32).astype(jnp.float32)
            scale = 1.0 / (4.0 * jnp.sqrt(block * count))
            out.append((prod[high] - prod[low]) * scale)
        return jnp.concatenate(out, axis=1)

    def sum_one(t, value):
        padded = jnp.concatenate([value, jnp.zeros((width, block - width), jnp.float32)], axis=1)
        g_src[t][...] = padded.reshape(n_group, gram_rows, block)
        g_one[t][me] = g_src[t][me]
        copies = [
            remote(g_src[t].at[beside(o)], g_one[t].at[me], sa.at[t, o], ra.at[t, o], (own, beside(o)))
            for o in range(1, n_group)
        ]
        for copy in copies:
            copy.start()
        return copies

    def sum_two(t, copies):
        for copy in copies:
            copy.wait_recv()
        total = g_one[t][0]
        for j in range(1, n_group):
            total = total + g_one[t][j]
        g_two[t][own] = total
        more = [
            remote(g_two[t].at[own], g_two[t].at[own], sb.at[t, o], rb.at[t, o], (up(o), me)) for o in doms
        ]
        for copy in more:
            copy.start()
        return more

    def sum_three(t, copies):
        for copy in copies:
            copy.wait_recv()
        total = g_two[t][0]
        for j in range(1, n_dom):
            total = total + g_two[t][j]
        g_all[t][me] = total * (1.0 / total_rows)
        more = [
            remote(g_all[t].at[me], g_all[t].at[me], sc.at[t, o], rc.at[t, o], (own, beside(o)))
            for o in range(1, n_group)
        ]
        for copy in more:
            copy.start()
        return more

    def sum_end(t, copies):
        for copy in copies:
            copy.wait_recv()
        return g_all[t][...].reshape(width, block)[:, :width]

    for load in smalls:
        load.wait()
    put_own(0, start_ref[...])
    pl.semaphore_wait(barrier, n_group - 1 + n_dom - 1)
    for copy in first_copies(0):
        copy.start()

    for c, load in enumerate(loads):
        load.wait()
        if c == n_chunks // 2:
            exchange_relay(0)

        def convert(i, carry):
            s = c * CHUNK + i
            tb[s] = (raw[s].astype(jnp.float32) - 7.5).astype(jnp.bfloat16)
            return carry

        lax.fori_loop(0, CHUNK, convert, 0)

    exchange_second(0)
    exchange_third(0)
    exchange_end(0)

    pending = []
    inverse = None
    for t in range(ITERS):
        image = apply_graph(t)
        if t > 0:
            image = dot(inverse, image, precision=HIGH)
        rounded = image.astype(jnp.bfloat16)
        put_own(t + 1, rounded)
        rounded_ref[...] = rounded
        one = sum_one(t, dot(rounded, rounded, ((1,), (1,))))
        for copy in first_copies(t + 1):
            copy.start()
        two = sum_two(t, one)
        exchange_relay(t + 1)
        three = sum_three(t, two)
        exchange_second(t + 1)
        state = factor_start(sum_end(t, three))
        state = factor_steps(state, 0, width // 2)
        exchange_third(t + 1)
        inverse = factor_end(factor_steps(state, width // 2, width))
        pending += one + two + three
        if t == ITERS - 1:
            vectors = dot(inverse, rounded_ref[...].astype(jnp.float32), precision=HIGH).astype(jnp.bfloat16)
            vec_ref[...] = vectors
        exchange_end(t + 1)

    final = dot(inverse, apply_graph(ITERS), precision=HIGH)
    local = dot(vec_ref[...].astype(jnp.float32), final, ((1,), (1,)), precision=HIGH)
    one = sum_one(ITERS, local)
    two = sum_two(ITERS, one)
    three = sum_three(ITERS, two)
    ritz_ref[...] = sum_end(ITERS, three)
    pending += one + two + three
    for copy in pending:
        copy.wait_send()
    for a in range(n_apply):
        exchange_sends(a)


def solution(mesh):
    n_dom, n_group = mesh.shape["dom"], mesh.shape["group"]
    n_apply = ITERS + 1

    def step(start, tiles, row_ptr, col_part, col_local, halo_list):
        width, rows_dev = start.shape
        slots, block = tiles.shape[1], tiles.shape[2]
        halo = halo_list.shape[2]
        in_part = rows_dev // block * n_group
        per = max(1, halo // n_group)
        gram_rows = width // n_group
        vmem = pl.BlockSpec(memory_space=pltpu.VMEM)
        dma = pltpu.SemaphoreType.DMA
        return pl.pallas_call(
            functools.partial(kernel, n_dom, n_group, halo, rows_dev * n_dom * n_group),
            out_shape=(
                jax.ShapeDtypeStruct((width, rows_dev), jnp.bfloat16),
                jax.ShapeDtypeStruct((width, width), jnp.float32),
            ),
            in_specs=[pl.BlockSpec(memory_space=pltpu.HBM)] * 6,
            out_specs=(vmem, vmem),
            scratch_shapes=(
                [
                    pltpu.VMEM(start.shape, start.dtype),
                    pltpu.SMEM(row_ptr.shape, jnp.int32),
                    pltpu.SMEM(col_part.shape, jnp.int32),
                    pltpu.SMEM(col_local.shape, jnp.int32),
                    pltpu.SMEM(halo_list.shape, jnp.int32),
                    dma((5,)),
                ]
                + [pltpu.VMEM((in_part, width, block), jnp.bfloat16)] * n_apply
                + [pltpu.VMEM((n_dom * halo, width, block), jnp.bfloat16)] * n_apply
                + [pltpu.VMEM((n_dom, per, width, block), jnp.bfloat16)] * n_apply
                + [
                    pltpu.VMEM((slots, block, block), jnp.int32),
                    pltpu.VMEM((slots, block, block), jnp.bfloat16),
                    pltpu.VMEM((slots + 1, width, block), jnp.float32),
                    pltpu.VMEM((width, rows_dev), jnp.bfloat16),
                ]
                + [pltpu.VMEM((n_group, gram_rows, block), jnp.float32)] * n_apply
                + [pltpu.VMEM((n_group, gram_rows, block), jnp.float32)] * n_apply
                + [pltpu.VMEM((n_dom, gram_rows, block), jnp.float32)] * n_apply
                + [pltpu.VMEM((n_group, gram_rows, block), jnp.float32)] * n_apply
                + [dma((slots // CHUNK,))]
                + [dma((n_apply, max(6, n_group)))] * 2
                + [dma((n_apply, n_dom))] * 2
                + [dma((n_apply, n_dom, n_group))] * 2
                + [dma((n_apply, n_group))] * 2
                + [dma((n_apply, n_dom))] * 2
                + [dma((n_apply, n_group))] * 2
            ),
            compiler_params=pltpu.CompilerParams(
                collective_id=0, has_side_effects=True, vmem_limit_bytes=67043328
            ),
        )(start, tiles, row_ptr, col_part, col_local, halo_list)

    return jax.shard_map(
        step,
        mesh=mesh,
        in_specs=(
            P(None, ("dom", "group")),
            P(("dom", "group"), None, None, None),
            P(("dom", "group"), None),
            P(("dom", "group"), None),
            P(("dom", "group"), None),
            P("dom", None, None),
        ),
        out_specs=(P(None, ("dom", "group")), P()),
        check_vma=False,
    )
```
